512 devices in a mesh: dp: 64 (over x, y, z_hi), head: 8 (over z_lo, core).
Axes of the slice: x: 4, y: 8, z: 8 (z_hi: 2, z_lo: 4; z = z_hi * 4 + z_lo), core: 2. Of those that a mesh axis runs over, the one named last changes fastest.
Arguments:
- tokens: bfloat16 [16384, 8192], P('dp', 'head'), may hold values from -6 to 6
- key_weight: bfloat16 [8192, 1024], P('dp', 'head'), may hold values from -0.0625 to 0.0625
- queries: bfloat16 [16384, 8192], P('dp', 'head'), may hold values from -51 to 51
- values: bfloat16 [16384, 1024], P('dp', 'head'), may hold values from -6 to 6
- out_grad: bfloat16 [16384, 8192], P('dp', 'head'), may hold values from -6 to 6
Outputs:
- query_grad: bfloat16 [16384, 8192], P('dp', 'head')
- value_grad: bfloat16 [16384, 1024], P('dp', 'head')
- weight_grad: float32 [8192, 1024], P('dp', 'head')
The draws below stay inside these ranges and needn't reach their ends.
All inputs are finite; a program needn't handle non-finite values.
Results may differ from the reference program's by a relative error of at most 0.022.
The reference program's roundings to bfloat16 on the way (of `keys`, `weights`, `out`, `dscores` and `key_grad`) count: a program that leaves them out, or rounds other values in their place, can miss the bound.
Values may be sent and summed in bfloat16 or wider, within the bound.
No kernel may reach another device: no remote copies, remote signals or barrier semaphores. Data moves between devices by JAX's collectives and lax.ppermute only.
A program may use at most 64 MiB of HBM per device.

```python
import jax
import jax.numpy as jnp
from jax import lax

D = 8192
HD = 128
GROUP = 8
LEN = 256
KVH = 8
SEQS = 64


def draw_queries(key, part):
    shape = (SEQS * LEN, KVH * GROUP * HD)
    base_key = jax.random.fold_in(key, 11)
    base = jnp.clip(jax.random.normal(base_key, shape, jnp.float32), -6.0, 6.0)
    return base.astype(jnp.bfloat16)


def block_levels(key, dims, shards, smallest, high):
    def one(position, blocks):
        steps = jax.random.uniform(jax.random.fold_in(jax.random.fold_in(key, 6), position), (blocks,), jnp.float32, smallest / len(shards), high / len(shards))
        return jnp.repeat(jnp.exp(steps), dims[position] // blocks).reshape((-1,) + (1,) * (len(dims) - position - 1))

    level = one(*shards[0])
    for cut in shards[1:]:
        level = level * one(*cut)
    return level


def noise(key, extent, spread, most, cuts=(), held_as=jnp.bfloat16):
    result = jax.random.normal(key, extent, jnp.float32) * spread
    if len(cuts) > 0:
        result = block_levels(key, extent, cuts, -0.22, 0.18) * result
    return jnp.clip(result, min=-most, max=most).astype(held_as)


def setup_inputs(seed: int = 0) -> dict:
    streams_of = jax.random.split(jax.random.key(seed), 6)
    return {
        "tokens": noise(streams_of[0], (SEQS * LEN, D), 1.0, 6.0, ((0, 64), (1, 8))),
        "key_weight": noise(streams_of[1], (D, KVH * HD), D ** -0.5, 0.0625, ((0, 64), (1, 8))),
        "queries": draw_queries(jax.random.fold_in(streams_of[5], 71), 0),
        "values": noise(streams_of[3], (SEQS * LEN, KVH * HD), 1.0, 6.0, ((0, 64), (1, 8))),
        "out_grad": noise(streams_of[4], (SEQS * LEN, KVH * GROUP * HD), 1.0, 6.0, ((0, 64), (1, 8))),
    }


def one_sequence(pieces):
    q, k, v, g = pieces
    qf = q.astype(jnp.float32)
    kf = k.astype(jnp.float32)
    vf = v.astype(jnp.float32)
    gf = g.astype(jnp.float32)
    scale = HD ** -0.5
    scores = jnp.einsum('qhgd,khd->hgqk', qf, kf) * scale
    rows = lax.broadcasted_iota(jnp.int32, (LEN, LEN), 0)
    cols = lax.broadcasted_iota(jnp.int32, (LEN, LEN), 1)
    keep = rows >= cols
    scores = jnp.where(keep, scores, jnp.float32(-1e30))
    top = jnp.max(scores, axis=-1, keepdims=True)
    expo = jnp.where(keep, jnp.exp(scores - top), jnp.float32(0.0))
    probs = expo / jnp.sum(expo, axis=-1, keepdims=True)
    weights = probs.astype(jnp.bfloat16)
    out = jnp.einsum('hgqk,khd->qhgd', weights.astype(jnp.float32), vf).astype(jnp.bfloat16)
    dprobs = jnp.einsum('qhgd,khd->hgqk', gf, vf)
    delta = jnp.transpose(jnp.sum(gf * out.astype(jnp.float32), axis=-1), (1, 2, 0))
    dscores = (probs * (dprobs - delta[..., None])).astype(jnp.bfloat16)
    dsf = dscores.astype(jnp.float32)
    dq = (jnp.einsum('hgqk,khd->qhgd', dsf, kf) * scale).astype(jnp.bfloat16)
    dk = (jnp.einsum('hgqk,qhgd->khd', dsf, qf) * scale).astype(jnp.bfloat16)
    dv = jnp.einsum('hgqk,qhgd->khd', weights.astype(jnp.float32), gf).astype(jnp.bfloat16)
    return dq, dk, dv


def reference(tokens, key_weight, queries, values, out_grad):
    heads = key_weight.shape[1] // HD
    keys = jnp.dot(tokens, key_weight, preferred_element_type=jnp.float32).astype(jnp.bfloat16)
    dq, dk, dv = lax.map(one_sequence, (queries.reshape(SEQS, LEN, heads, GROUP, HD), keys.reshape(SEQS, LEN, heads, HD), values.reshape(SEQS, LEN, heads, HD), out_grad.reshape(SEQS, LEN, heads, GROUP, HD)))
    key_grad = dk.reshape(SEQS * LEN, heads * HD)
    weight_grad = lax.dot_general(tokens, key_grad, (((0,), (0,)), ((), ())), preferred_element_type=jnp.float32)
    return dq.reshape(SEQS * LEN, heads * GROUP * HD), dv.reshape(SEQS * LEN, heads * HD), weight_grad
```

```python
import jax
import jax.numpy as jnp
from jax import lax
from jax.sharding import PartitionSpec as P

X, Y, ZH, ZL, C = 4, 8, 2, 4, 2


def dp_of(x, y, zh):
    return ((x % X) * Y + y) * ZH + zh


def place(x, y, zh, zl, c):
    return dp_of(x, y, zh) * ZL * C + (zl % ZL) * C + c


CHIPS = [
    (x, y, zh, zl, c)
    for x in range(X)
    for y in range(Y)
    for zh in range(ZH)
    for zl in range(ZL)
    for c in range(C)
]
ALONG_X = [[dp_of(x, y, zh) for x in range(X)] for y in range(Y) for zh in range(ZH)]
ALONG_YZ = [[dp_of(x, y, zh) for y in range(Y) for zh in range(ZH)] for x in range(X)]
CORES = [(h, h ^ 1) for h in range(ZL * C)]


def turned(j):
    return [(place(x, y, zh, zl, c), place(zl, y, zh, x + j, c)) for x, y, zh, zl, c in CHIPS]


def spread(block, groups):
    n = len(groups[0])
    many = jnp.broadcast_to(block[None], (n,) + block.shape)
    return lax.all_to_all(many, "dp", 0, 0, tiled=True, axis_index_groups=groups)


def reorder(parts, zl):
    back = parts[::-1]
    twice = jnp.concatenate([back, back], axis=0)
    return lax.dynamic_slice_in_dim(twice, X - 1 - zl, X, axis=0)


def attention(queries, keys, values, out_grad):
    width = values.shape[1]
    length = queries.shape[0]
    group = queries.shape[1] // width
    scale = width ** (-0.5)
    query_heads = queries.reshape(length, group, width)
    grad_heads = out_grad.reshape(length, group, width)
    scores = (
        jnp.einsum("qgd,kd->gqk", query_heads, keys, preferred_element_type=jnp.float32) * scale
    )
    rows = lax.broadcasted_iota(jnp.int32, (length, length), 0)
    cols = lax.broadcasted_iota(jnp.int32, (length, length), 1)
    keep = rows >= cols
    scores = jnp.where(keep, scores, jnp.float32(-1e30))
    top = jnp.max(scores, axis=-1, keepdims=True)
    expo = jnp.where(keep, jnp.exp(scores - top), jnp.float32(0.0))
    probs = expo / jnp.sum(expo, axis=-1, keepdims=True)
    weights = probs.astype(jnp.bfloat16)
    attended = jnp.einsum(
        "gqk,kd->qgd", weights, values, preferred_element_type=jnp.float32
    ).astype(jnp.bfloat16)
    dprobs = jnp.einsum("qgd,kd->gqk", grad_heads, values, preferred_element_type=jnp.float32)
    delta = jnp.transpose(
        jnp.sum(grad_heads.astype(jnp.float32) * attended.astype(jnp.float32), axis=-1), (1, 0)
    )
    dscores = (probs * (dprobs - delta[..., None])).astype(jnp.bfloat16)
    query_grad = (
        jnp.einsum("gqk,kd->qgd", dscores, keys, preferred_element_type=jnp.float32) * scale
    ).astype(jnp.bfloat16)
    key_grad = (
        jnp.einsum("gqk,qgd->kd", dscores, query_heads, preferred_element_type=jnp.float32) * scale
    ).astype(jnp.bfloat16)
    value_grad = jnp.einsum(
        "gqk,qgd->kd", weights, grad_heads, preferred_element_type=jnp.float32
    ).astype(jnp.bfloat16)
    return query_grad.reshape(length, group * width), key_grad, value_grad


def on_device(tokens, key_weight, queries, values, out_grad):
    f32 = jnp.float32
    length, feats = tokens.shape
    head = lax.axis_index("head")
    zl, c = head // C, head % C
    mine = [lax.ppermute(tokens, ("dp", "head"), turned(j)) for j in range(X)]
    weight = spread(key_weight, ALONG_YZ).reshape(C * feats, -1)
    width = weight.shape[1]
    theirs = [lax.ppermute(block, "head", CORES) for block in mine]
    near = lax.dynamic_slice_in_dim(weight, c * feats, feats, axis=0)
    far = lax.dynamic_slice_in_dim(weight, (1 - c) * feats, feats, axis=0)
    partial = jnp.stack(
        [
            jnp.dot(a, near, preferred_element_type=f32) + jnp.dot(b, far, preferred_element_type=f32)
            for a, b in zip(mine, theirs)
        ]
    )
    partial = lax.all_to_all(
        reorder(partial, zl), "dp", 0, 0, tiled=True, axis_index_groups=ALONG_X
    )
    keys = jnp.sum(partial, axis=0).astype(jnp.bfloat16)
    query_grad, key_grad, value_grad = attention(queries, keys, values, out_grad)
    grads = reorder(spread(key_grad, ALONG_X).reshape(X, length, width), zl)

    def contracted(blocks):
        return sum(
            lax.dot_general(
                a, grads[j], (((0,), (0,)), ((), ())), preferred_element_type=f32
            )
            for j, a in enumerate(blocks)
        )

    own, other = contracted(mine), contracted(theirs)
    rows = jnp.concatenate([own, other, own], axis=0).astype(jnp.bfloat16)
    rows = lax.dynamic_slice_in_dim(rows, c * feats, C * feats, axis=0)
    rows = lax.all_to_all(
        rows.reshape(Y * ZH, -1, width), "dp", 0, 0, tiled=True, axis_index_groups=ALONG_YZ
    )
    weight_grad = jnp.sum(rows.astype(f32), axis=0)
    return query_grad, value_grad, weight_grad


def solution(mesh):
    placed = (P("dp", "head"), P("dp", "head"), P("dp", "head"), P("dp", "head"), P("dp", "head"))
    return jax.shard_map(
        on_device,
        mesh=mesh,
        in_specs=placed,
        out_specs=(P("dp", "head"), P("dp", "head"), P("dp", "head")),
        check_vma=False,
    )
```

```python
import jax
import jax.numpy as jnp
from jax import lax
from jax.sharding import PartitionSpec as P

X, Y, ZH, ZL, C = 4, 8, 2, 4, 2


def dp_of(x, y, zh):
    return ((x % X) * Y + y) * ZH + zh


def place(x, y, zh, zl, c):
    return dp_of(x, y, zh) * ZL * C + (zl % ZL) * C + c


CHIPS = [
    (x, y, zh, zl, c)
    for x in range(X)
    for y in range(Y)
    for zh in range(ZH)
    for zl in range(ZL)
    for c in range(C)
]
CORES = [(h, h ^ 1) for h in range(ZL * C)]


ALONG_Y = [[dp_of(x, y, zh) for y in range(Y)] for x in range(X) for zh in range(ZH)]
BOTH = ("dp", "head")


def along_x(d):
    return [(place(x, y, zh, zl, c), place(x + d, y, zh, zl, c)) for x, y, zh, zl, c in CHIPS]


def to_owner(k):
    return [(place(x, y, zh, zl, c), place(zl + k, y, zh, x, c)) for x, y, zh, zl, c in CHIPS]


def from_owner(k):
    return [(b, a) for a, b in to_owner(k)]


def turned(flip):
    return [(place(x, y, zh, zl, c), place(zl, y, zh ^ flip, x, c)) for x, y, zh, zl, c in CHIPS]


def send(block, pairs):
    return lax.ppermute(block, BOTH, pairs)


def reorder(parts, first):
    back = parts[::-1]
    twice = jnp.concatenate([back, back], axis=0)
    return lax.dynamic_slice_in_dim(twice, X - 1 - first, X, axis=0)


def in_order(own, other, position):
    return jnp.where(position == 0, jnp.stack([own, other]), jnp.stack([other, own]))


def attention(queries, keys, values, out_grad):
    width = values.shape[1]
    length = queries.shape[0]
    group = queries.shape[1] // width
    scale = width ** (-0.5)
    query_heads = queries.reshape(length, group, width)
    grad_heads = out_grad.reshape(length, group, width)
    scores = (
        jnp.einsum("qgd,kd->gqk", query_heads, keys, preferred_element_type=jnp.float32) * scale
    )
    rows = lax.broadcasted_iota(jnp.int32, (length, length), 0)
    cols = lax.broadcasted_iota(jnp.int32, (length, length), 1)
    keep = rows >= cols
    scores = jnp.where(keep, scores, jnp.float32(-1e30))
    top = jnp.max(scores, axis=-1, keepdims=True)
    expo = jnp.where(keep, jnp.exp(scores - top), jnp.float32(0.0))
    probs = expo / jnp.sum(expo, axis=-1, keepdims=True)
    weights = probs.astype(jnp.bfloat16)
    attended = jnp.einsum(
        "gqk,kd->qgd", weights, values, preferred_element_type=jnp.float32
    ).astype(jnp.bfloat16)
    dprobs = jnp.einsum("qgd,kd->gqk", grad_heads, values, preferred_element_type=jnp.float32)
    delta = jnp.transpose(
        jnp.sum(grad_heads.astype(jnp.float32) * attended.astype(jnp.float32), axis=-1), (1, 0)
    )
    dscores = (probs * (dprobs - delta[..., None])).astype(jnp.bfloat16)
    query_grad = (
        jnp.einsum("gqk,kd->qgd", dscores, keys, preferred_element_type=jnp.float32) * scale
    ).astype(jnp.bfloat16)
    key_grad = (
        jnp.einsum("gqk,qgd->kd", dscores, query_heads, preferred_element_type=jnp.float32) * scale
    ).astype(jnp.bfloat16)
    value_grad = jnp.einsum(
        "gqk,qgd->kd", weights, grad_heads, preferred_element_type=jnp.float32
    ).astype(jnp.bfloat16)
    return query_grad.reshape(length, group * width), key_grad, value_grad


def on_device(tokens, key_weight, queries, values, out_grad):
    f32, bf16 = jnp.float32, jnp.bfloat16
    length, feats = tokens.shape
    rows, width = key_weight.shape
    dp, head = lax.axis_index("dp"), lax.axis_index("head")
    x, zh = dp // (Y * ZH), dp % ZH
    zl, c = head // C, head % C
    first = (x - zl) % X

    weight = in_order(*(send(key_weight, turned(flip)) for flip in range(ZH)), zh)
    mine = [tokens] + [send(tokens, along_x(d)) for d in range(1, X)]
    weight = jnp.broadcast_to(weight[None], (Y, ZH, rows, width))
    weight = lax.all_to_all(weight, "dp", 0, 0, tiled=True, axis_index_groups=ALONG_Y)
    weight = weight.reshape(C * feats, width)
    theirs = [lax.ppermute(block, "head", CORES) for block in mine]
    near = lax.dynamic_slice_in_dim(weight, c * feats, feats, axis=0)
    far = lax.dynamic_slice_in_dim(weight, (1 - c) * feats, feats, axis=0)
    partial = jnp.stack(
        [
            jnp.dot(a, near, preferred_element_type=f32) + jnp.dot(b, far, preferred_element_type=f32)
            for a, b in zip(mine, theirs)
        ]
    )
    partial = reorder(partial, first)
    keys = sum(send(partial[k], to_owner(k)) for k in range(X)).astype(bf16)
    query_grad, key_grad, value_grad = attention(queries, keys, values, out_grad)
    grads = reorder(jnp.stack([send(key_grad, from_owner(k)) for k in range(X)]), first)

    def contracted(blocks):
        return sum(
            lax.dot_general(
                a, grads[d], (((0,), (0,)), ((), ())), preferred_element_type=f32
            )
            for d, a in enumerate(blocks)
        )

    own, other = contracted(mine), contracted(theirs)
    total = jnp.concatenate([own, other, own], axis=0).astype(bf16)
    total = lax.dynamic_slice_in_dim(total, c * feats, C * feats, axis=0)
    total = lax.all_to_all(
        total.reshape(Y, ZH * rows, width), "dp", 0, 0, tiled=True, axis_index_groups=ALONG_Y
    )
    total = jnp.sum(total.astype(f32), axis=0).astype(bf16).reshape(ZH, rows, width)
    stays = lax.dynamic_index_in_dim(total, zh, 0, keepdims=False)
    leaves = lax.dynamic_index_in_dim(total, 1 - zh, 0, keepdims=False)
    weight_grad = send(stays, turned(0)).astype(f32) + send(leaves, turned(1)).astype(f32)
    return query_grad, value_grad, weight_grad


def solution(mesh):
    placed = (P("dp", "head"), P("dp", "head"), P("dp", "head"), P("dp", "head"), P("dp", "head"))
    return jax.shard_map(
        on_device,
        mesh=mesh,
        in_specs=placed,
        out_specs=(P("dp", "head"), P("dp", "head"), P("dp", "head")),
        check_vma=False,
    )
```

```python
import jax
import jax.numpy as jnp
from jax import lax
from jax.sharding import PartitionSpec as P

X, Y, ZH, U, V, C = 4, 8, 2, 2, 2, 2
HALF = Y // 2
BOTH = ("dp", "head")


def dp_of(x, y, zh):
    return (x * Y + y) * ZH + zh


def place(x, y, zh, u, v, c):
    return dp_of(x, y, zh) * U * V * C + (u * V + v) * C + c


DEVICES = [
    (x, y, zh, u, v, c)
    for x in range(X)
    for y in range(Y)
    for zh in range(ZH)
    for u in range(U)
    for v in range(V)
    for c in range(C)
]
ALONG_Y = [[dp_of(x, y, zh) for y in range(Y)] for x in range(X) for zh in range(ZH)]
ALONG_XV = [
    [place(x, y, zh, u, v, c) for x in range(X) for v in range(V)]
    for y in range(Y)
    for zh in range(ZH)
    for u in range(U)
    for c in range(C)
]
CORES = [(h, h ^ 1) for h in range(U * V * C)]


def to_features(j):
    return [
        (place(x, y, zh, u, v, c), place(u * V + v, y, zh, (x % 2) ^ j, c, x // 2))
        for x, y, zh, u, v, c in DEVICES
    ]


def to_owner(flip):
    return [
        (place(x, y, zh, u, v, c), place(x, v * HALF + y % HALF, zh ^ flip, u, y // HALF, c))
        for x, y, zh, u, v, c in DEVICES
    ]


def spread(block, axis, groups):
    n = len(groups[0])
    many = jnp.broadcast_to(block[None], (n,) + block.shape)
    return lax.all_to_all(many, axis, 0, 0, tiled=True, axis_index_groups=groups)


def in_order(own, other, position):
    return jnp.where(position == 0, jnp.stack([own, other]), jnp.stack([other, own]))


def sequences(parts, first):
    low = [jnp.where(first % 2 == 0, parts[i], parts[i ^ 1]) for i in range(X)]
    return [jnp.where(first // 2 == 0, low[i], low[i ^ 2]) for i in range(X)]


def attention(queries, keys, values, out_grad):
    width = values.shape[1]
    length = queries.shape[0]
    group = queries.shape[1] // width
    scale = width ** (-0.5)
    query_heads = queries.reshape(length, group, width)
    grad_heads = out_grad.reshape(length, group, width)
    scores = (
        jnp.einsum("qgd,kd->gqk", query_heads, keys, preferred_element_type=jnp.float32) * scale
    )
    rows = lax.broadcasted_iota(jnp.int32, (length, length), 0)
    cols = lax.broadcasted_iota(jnp.int32, (length, length), 1)
    keep = rows >= cols
    scores = jnp.where(keep, scores, jnp.float32(-1e30))
    top = jnp.max(scores, axis=-1, keepdims=True)
    expo = jnp.where(keep, jnp.exp(scores - top), jnp.float32(0.0))
    probs = expo / jnp.sum(expo, axis=-1, keepdims=True)
    weights = probs.astype(jnp.bfloat16)
    attended = jnp.einsum(
        "gqk,kd->qgd", weights, values, preferred_element_type=jnp.float32
    ).astype(jnp.bfloat16)
    dprobs = jnp.einsum("qgd,kd->gqk", grad_heads, values, preferred_element_type=jnp.float32)
    delta = jnp.transpose(
        jnp.sum(grad_heads.astype(jnp.float32) * attended.astype(jnp.float32), axis=-1), (1, 0)
    )
    dscores = (probs * (dprobs - delta[..., None])).astype(jnp.bfloat16)
    query_grad = (
        jnp.einsum("gqk,kd->qgd", dscores, keys, preferred_element_type=jnp.float32) * scale
    ).astype(jnp.bfloat16)
    key_grad = (
        jnp.einsum("gqk,qgd->kd", dscores, query_heads, preferred_element_type=jnp.float32) * scale
    ).astype(jnp.bfloat16)
    value_grad = jnp.einsum(
        "gqk,qgd->kd", weights, grad_heads, preferred_element_type=jnp.float32
    ).astype(jnp.bfloat16)
    return query_grad.reshape(length, group * width), key_grad, value_grad


def step(tokens, key_weight, queries, values, out_grad):
    f32, bf16 = jnp.float32, jnp.bfloat16
    length, feats = tokens.shape
    rows, width = key_weight.shape
    dp, head = lax.axis_index("dp"), lax.axis_index("head")
    zh, u, c = dp % ZH, head // (V * C), head % C
    first = 2 * c + u
    weight = []
    for flip in range(ZH):
        weight.append(lax.ppermute(key_weight, BOTH, to_owner(flip)))
    blocks = []
    for j in range(U):
        blocks.append(lax.ppermute(tokens, BOTH, to_features(j)))
    weight = in_order(*weight, zh)
    weight = spread(weight, "dp", ALONG_Y).reshape(V, feats, width)
    blocks += [lax.ppermute(block, "head", CORES) for block in blocks]
    partial = [
        jnp.stack([jnp.dot(a, weight[v], preferred_element_type=f32) for v in range(V)])
        for a in blocks
    ]
    partial = jnp.stack(sequences(partial, first)).reshape(X * V, length, width)
    partial = lax.all_to_all(partial, BOTH, 0, 0, tiled=True, axis_index_groups=ALONG_XV)
    keys = jnp.sum(partial, axis=0).astype(bf16)
    query_grad, key_grad, value_grad = attention(queries, keys, values, out_grad)
    grads = spread(key_grad, BOTH, ALONG_XV).reshape(X, V, length, width)
    grads = sequences([grads[i] for i in range(X)], first)
    total = jnp.stack(
        [
            sum(
                lax.dot_general(
                    a, g[v], (((0,), (0,)), ((), ())), preferred_element_type=f32
                )
                for a, g in zip(blocks, grads)
            ).astype(bf16)
            for v in range(V)
        ]
    )
    total = lax.all_to_all(
        total.reshape(Y, ZH * rows, width), "dp", 0, 0, tiled=True, axis_index_groups=ALONG_Y
    )
    total = jnp.sum(total.astype(f32), axis=0).astype(bf16).reshape(ZH, rows, width)
    stays = lax.dynamic_index_in_dim(total, zh, 0, keepdims=False)
    leaves = lax.dynamic_index_in_dim(total, 1 - zh, 0, keepdims=False)
    weight_grad = lax.ppermute(stays, BOTH, to_owner(0)).astype(f32)
    weight_grad += lax.ppermute(leaves, BOTH, to_owner(1)).astype(f32)
    return query_grad, value_grad, weight_grad


def solution(mesh):
    placed = (P("dp", "head"), P("dp", "head"), P("dp", "head"), P("dp", "head"), P("dp", "head"))
    return jax.shard_map(
        step,
        mesh=mesh,
        in_specs=placed,
        out_specs=(P("dp", "head"), P("dp", "head"), P("dp", "head")),
        check_vma=False,
    )
```
